32 devices in a mesh: vessel: 2 (over core), gather: 16 (over z, y, x).
Axes of the slice: x: 2, y: 2, z: 4, core: 2. Of those that a mesh axis runs over, the one named last changes fastest.
Arguments:
- observed: bfloat16 [16, 16, 2048], P('gather'), may hold values from -6 to 6
- estimate: bfloat16 [2, 16, 16, 2048], P('vessel', 'gather'), may hold values from -6 to 6
- delays: int32 [2, 16], P('vessel', 'gather'), may hold values from 0 to 256
- taps_time: float32 [16, 7], replicated, may hold values from -2 to 2
- taps_shot: float32 [16, 7], replicated, may hold values from -0.5 to 0.5
- thresh: float32 [16], replicated, may hold values from 0.02 to 0.3
Outputs:
- deblended: bfloat16 [2, 16, 16, 2048], P('vessel', 'gather')
The draws below stay inside these ranges and needn't reach their ends.
All inputs are finite; a program needn't handle non-finite values.
Results may differ from the reference program's by a relative error of at most 0.022.
Values may be sent and summed in bfloat16 or wider, within the bound.
A program may use at most 64 MiB of HBM per device.

```python
import math
import jax
import jax.numpy as jnp
from jax import lax

TT = 2048
CH = 16
TAPS = 7
TIME_SPACING = 4
SHOT_SPACING = 2
MAXD = 256
ITERS = 2
VES = 2
SHOTS = 16
REC = 16


def with_ends(array, rng, least, largest):
    extent = array.shape
    spot = [jax.random.randint(jax.random.fold_in(rng, axis), (), 0, extent[axis]) for axis in range(len(extent))]
    array = array.at[tuple(spot)].set(least)
    longest = extent.index(max(extent))
    spot[longest] = (spot[longest] + 1) % extent[longest]
    return array.at[tuple(spot)].set(largest)


def block_scale(key, shape, shards, smallest, largest):
    gain = 1.0
    for axis_at, blocks in shards:
        draws = jax.random.uniform(jax.random.fold_in(jax.random.fold_in(key, 6), axis_at), (blocks,), jnp.float32, smallest / len(shards), largest / len(shards))
        gain = gain * jnp.repeat(jnp.exp(draws), shape[axis_at] // blocks).reshape((-1,) + (1,) * (len(shape) - 1 - axis_at))
    return gain


def scatter_about(stream_key, dims, deviation, most, shards=(), held_as=jnp.bfloat16):
    loudness = block_scale(stream_key, dims, shards, -0.22, 0.18) if shards else 1.0
    result = jax.random.normal(stream_key, dims, jnp.float32) * deviation * loudness
    return jnp.minimum(jnp.maximum(result, -most), most).astype(held_as)


def setup_inputs(seed: int = 0) -> dict:
    keys = jax.random.split(jax.random.key(seed), 7)
    observed = scatter_about(keys[0], (SHOTS, REC, TT), 1.0, 6.0, ((0, 16),))
    estimate = scatter_about(keys[1], (VES, SHOTS, REC, TT), 0.7, 6.0, ((0, 2), (1, 16)))
    delays = with_ends(jax.random.randint(keys[2], (VES, SHOTS), 0, MAXD + 1), jax.random.fold_in(keys[2], 1), 0, MAXD).astype(jnp.int32)
    taps_time = scatter_about(keys[3], (CH, TAPS), TAPS ** -0.5, 2.0, (), jnp.float32)
    taps_shot = scatter_about(keys[4], (CH, TAPS), (TAPS * CH) ** -0.5, 0.5, (), jnp.float32)
    thresh = jnp.clip(jnp.exp(jax.random.uniform(keys[5], (CH,), jnp.float32, math.log(0.02), math.log(0.3))), 0.02, 0.3)
    return {"observed": observed, "estimate": estimate, "delays": delays, "taps_time": taps_time, "taps_shot": taps_shot, "thresh": thresh}


def late_shift(traces, shift_by):
    padded = jnp.pad(traces, ((0, 0), (0, 0), (MAXD, MAXD)))

    def single(trace, shift_amount):
        return lax.dynamic_slice_in_dim(trace, (MAXD - shift_amount).astype(jnp.int32), TT, 1)

    return jax.vmap(single)(padded, shift_by)


def early_shift(traces, shift_by):
    padded = jnp.pad(traces, ((0, 0), (0, 0), (MAXD, MAXD)))

    def single(trace, shift_amount):
        return lax.dynamic_slice_in_dim(trace, (MAXD + shift_amount).astype(jnp.int32), TT, 1)

    return jax.vmap(single)(padded, shift_by)


def along_time(field, taps, shift_sign):
    filter_reach = 3 * TIME_SPACING
    length = field.shape[3]
    padded = jnp.pad(field, ((0, 0), (0, 0), (0, 0), (filter_reach, filter_reach)))
    total = jnp.zeros((taps.shape[0],) + field.shape[1:], jnp.float32)
    for tap_index in range(-3, 4):
        start_offset = filter_reach + shift_sign * tap_index * TIME_SPACING
        total = total + taps[:, tap_index + 3][:, None, None, None] * padded[:, :, :, start_offset:start_offset + length]
    return total


def along_shots(field, taps, shift_sign):
    filter_reach = 3 * SHOT_SPACING
    length = field.shape[1]
    padded = jnp.pad(field, ((0, 0), (filter_reach, filter_reach), (0, 0), (0, 0)))
    total = jnp.zeros((taps.shape[0],) + field.shape[1:], jnp.float32)
    for tap_index in range(-3, 4):
        start_offset = filter_reach + shift_sign * tap_index * SHOT_SPACING
        total = total + taps[:, tap_index + 3][:, None, None, None] * padded[:, start_offset:start_offset + length]
    return total


def shrink_filter(plane, taps_time, taps_shot, thresh):
    field = plane.astype(jnp.float32)[None]
    group_time = taps_time.reshape(-1, 4, taps_time.shape[1])
    group_shot = taps_shot.reshape(-1, 4, taps_shot.shape[1])
    group_thresh = thresh.reshape(-1, 4)

    def channel(carry, pieces):
        time_taps, shot_taps, limits = pieces
        forward_pass = along_shots(along_time(field, time_taps, 1), shot_taps, 1)
        bound = limits[:, None, None, None]
        shrunk = forward_pass - jnp.clip(forward_pass, -bound, bound)
        back = along_time(along_shots(shrunk, shot_taps, -1), time_taps, -1)
        return carry + jnp.sum(back, axis=0), None

    total, _ = lax.scan(channel, jnp.zeros(plane.shape, jnp.float32), (group_time, group_shot, group_thresh))
    return total.astype(jnp.bfloat16)


def reference(observed, estimate, delays, taps_time, taps_shot, thresh):
    current = estimate
    for step in range(ITERS):
        blend = jnp.zeros(observed.shape, jnp.float32)
        for vessel_index in range(VES):
            blend = blend + late_shift(current[vessel_index], delays[vessel_index]).astype(jnp.float32)
        resid = observed.astype(jnp.float32) - blend
        updated = []
        for vessel_index in range(VES):
            plane = (current[vessel_index].astype(jnp.float32) + early_shift(resid, delays[vessel_index])).astype(jnp.bfloat16)
            updated.append(shrink_filter(plane, taps_time, taps_shot, thresh))
        current = jnp.stack(updated)
    return current
```

```python
import functools

import jax
import jax.numpy as jnp
from jax import lax
from jax.experimental import pallas as pl
from jax.experimental.pallas import tpu as pltpu
from jax.sharding import PartitionSpec as P

TIME_SPACING = 4
SHOT_SPACING = 2
MAXD = 256
ITERS = 2
LANES = 128
REACH = 3

MESH = pl.DeviceIdType.MESH


def shift_left(padded, amount, width, top):
    current = padded
    step = top
    keep = top
    while step >= LANES:
        bit = (amount & step) != 0
        current = jnp.where(bit, current[:, step : step + width + keep], current[:, : width + keep])
        step //= 2
        keep = step
    extent = width + LANES
    current = current[:, :extent]
    while step >= 1:
        bit = (amount & step) != 0
        current = jnp.where(bit, pltpu.roll(current, extent - step, 1), current)
        step //= 2
    return current[:, :width]


def kernel(
    dims,
    x_ref,
    obs_ref,
    d_ref,
    tt_ref,
    ts_ref,
    th_ref,
    out_ref,
    flat,
    flat2,
    stage,
    rbuf,
    dsend,
    drecv,
    m_s,
    mt_s,
    th_s,
    pst,
    g_s,
    tail_s,
    tail_r,
    stage2,
    rbuf2,
    s_pay,
    r_pay,
    s_del,
    r_del,
    s_tail,
    r_tail,
    s_out,
    r_out,
):
    n, width, channels, taps, chunks, rows, depth = dims
    v = lax.axis_index("vessel")
    me = lax.axis_index("gather")
    other = 1 - v
    nt = width // LANES
    group = rows // n

    barrier = pltpu.get_barrier_semaphore()

    def greet(i, carry):
        p = lax.rem(me + i, n)
        pl.semaphore_signal(barrier, inc=1, device_id=(v, p), device_id_type=MESH)
        pl.semaphore_signal(barrier, inc=1, device_id=(other, p), device_id_type=MESH)
        return carry

    lax.fori_loop(1, n, greet, 0)
    pl.semaphore_signal(barrier, inc=1, device_id=(other, me), device_id_type=MESH)

    def to_rows(ref, value):
        for i in range(nt):
            ref[pl.ds(i, n, stride=nt), :] = value[:, i * LANES : (i + 1) * LANES]

    def from_rows(ref):
        return jnp.concatenate([ref[pl.ds(i, n, stride=nt), :] for i in range(nt)], axis=1)

    to_rows(flat, x_ref[0, 0].astype(jnp.float32))
    to_rows(flat2, obs_ref[0].astype(jnp.float32))
    stage[:, 0] = flat[...].reshape(n, nt, LANES).astype(jnp.bfloat16)
    stage[:, 1] = flat2[...].reshape(n, nt, LANES).astype(jnp.bfloat16)
    dsend[...] = jnp.broadcast_to(d_ref[...], (1, LANES))

    pl.semaphore_wait(barrier, 2 * n - 1)

    def payload(p, send_at, recv_at, slot):
        return pltpu.make_async_remote_copy(
            src_ref=stage.at[p],
            dst_ref=rbuf.at[slot],
            send_sem=s_pay.at[send_at],
            recv_sem=r_pay.at[recv_at],
            device_id=(v, p),
            device_id_type=MESH,
        )

    def delay(to_vessel, p, side, send_at, vessel_at, shot_at):
        return pltpu.make_async_remote_copy(
            src_ref=dsend,
            dst_ref=drecv.at[vessel_at, shot_at],
            send_sem=s_del.at[side, send_at],
            recv_sem=r_del.at[vessel_at, shot_at],
            device_id=(to_vessel, p),
            device_id_type=MESH,
        )

    delay(other, me, 1, 0, v, me).start()

    def send(i, carry):
        p = lax.rem(me + i, n)
        payload(p, i, me, me).start()
        delay(v, p, 0, i, v, me).start()
        delay(other, p, 1, i, v, me).start()
        return carry

    lax.fori_loop(1, n, send, 0)
    rbuf[me] = stage[me]
    drecv[v, me] = dsend[...]

    def build(q, carry):
        row_ch = q * group + lax.broadcasted_iota(jnp.int32, (rows, channels), 0) // n
        pick = row_ch == lax.broadcasted_iota(jnp.int32, (rows, channels), 1)
        pick_f = pick.astype(jnp.float32)
        tt = jnp.dot(pick_f, tt_ref[...], precision=lax.Precision.HIGHEST, preferred_element_type=jnp.float32)
        ts = jnp.dot(pick_f, ts_ref[...], precision=lax.Precision.HIGHEST, preferred_element_type=jnp.float32)
        th_s[q] = jnp.sum(jnp.where(pick, th_ref[...], 0.0), axis=1, keepdims=True)
        col = lax.broadcasted_iota(jnp.int32, (rows, depth), 1)
        row = lax.broadcasted_iota(jnp.int32, (rows, depth), 0)
        apart = lax.rem(col, n) - lax.rem(row, n)
        tap_of = col // n
        a = jnp.zeros((rows, depth), jnp.float32)
        b = jnp.zeros((rows, depth), jnp.float32)
        for k in range(taps):
            a = jnp.where(tap_of == k, tt[:, k : k + 1], a)
            b = jnp.where(apart == (k - REACH) * SHOT_SPACING, ts[:, k : k + 1], b)
        m = a * b
        m_s[q] = m.astype(jnp.bfloat16)
        mt_s[q] = m.T.astype(jnp.bfloat16)
        return carry

    if chunks == 1:
        build(0, 0)
    else:
        lax.fori_loop(0, chunks, build, 0)
    if depth > taps * n:
        pst[taps * n :, :] = jnp.zeros((depth - taps * n, width), jnp.bfloat16)

    def arrive(i, carry):
        p = lax.rem(me + i, n)
        payload(p, i, p, p).wait_recv()
        delay(v, p, 0, i, v, p).wait_recv()
        delay(v, p, 0, i, other, p).wait_recv()
        return carry

    delay(other, me, 1, 0, other, me).wait_recv()
    lax.fori_loop(1, n, arrive, 0)

    flat[...] = rbuf[:, 0].astype(jnp.float32).reshape(n * nt, LANES)
    flat2[...] = rbuf[:, 1].astype(jnp.float32).reshape(n * nt, LANES)
    held = from_rows(flat)
    observed = from_rows(flat2)
    d_mine = drecv[v].reshape(n, LANES)[:, :1]
    d_other = drecv[other].reshape(n, LANES)[:, :1]

    early_mark = width - 2 * MAXD
    blocks = [(0, early_mark), (early_mark, width)]
    block_width = 512

    def filter_columns(start, stop):
        def one(q, first):
            for c0 in range(start, stop, block_width):
                c1 = min(c0 + block_width, stop)
                y = jnp.dot(m_s[q], pst[:, c0:c1], preferred_element_type=jnp.float32)
                th = th_s[q]
                z = (y - jnp.minimum(jnp.maximum(y, -th), th)).astype(jnp.bfloat16)
                g = jnp.dot(mt_s[q], z, preferred_element_type=jnp.float32)
                if first:
                    g_s[:, c0:c1] = g
                else:
                    g_s[:, c0:c1] += g

        one(0, True)
        if chunks > 1:

            def more(q, carry):
                one(q, False)
                return carry

            lax.fori_loop(1, chunks, more, 0)

    def stack_taps(piece, lead, start, stop):
        extent = piece.shape[1]
        for k in range(taps):
            step = (k - REACH) * TIME_SPACING
            moved = piece if step == 0 else pltpu.roll(piece, (extent - step) % extent, 1)
            pst[k * n : (k + 1) * n, start:stop] = moved[:, lead : lead + stop - start].astype(jnp.bfloat16)

    zeros = lambda w: jnp.zeros((n, w), jnp.float32)

    def tail_copy(it):
        return pltpu.make_async_remote_copy(
            src_ref=tail_s.at[it],
            dst_ref=tail_r.at[it],
            send_sem=s_tail.at[it],
            recv_sem=r_tail.at[it],
            device_id=(other, me),
            device_id_type=MESH,
        )

    for it in range(ITERS):
        d_held, d_plane = (d_mine, d_other) if it % 2 == 0 else (d_other, d_mine)
        tail_s[it] = held[:, width - MAXD :].astype(jnp.bfloat16)
        tail_copy(it).start()
        seen = shift_left(jnp.concatenate([observed, zeros(2 * MAXD)], axis=1), d_plane, width, MAXD)
        crossed = shift_left(
            jnp.concatenate([zeros(MAXD), held, zeros(3 * MAXD)], axis=1),
            d_plane - d_held + MAXD,
            width,
            2 * MAXD,
        )
        plane = seen - crossed
        stack_taps(
            jnp.concatenate([plane[:, : early_mark + LANES], zeros(LANES)], axis=1), 0, 0, early_mark
        )
        filter_columns(0, early_mark)
        tail_copy(it).wait_recv()
        cut = width - MAXD
        time = cut + lax.broadcasted_iota(jnp.int32, (n, MAXD), 1)
        end = jnp.where(time + d_plane < width, plane[:, cut:], tail_r[it].astype(jnp.float32))
        stack_taps(
            jnp.concatenate([plane[:, early_mark - LANES : cut], end, zeros(LANES)], axis=1),
            LANES,
            early_mark,
            width,
        )
        filter_columns(early_mark, width)
        total = zeros(width)
        for k in range(taps):
            step = (k - REACH) * TIME_SPACING
            g = g_s[k * n : (k + 1) * n, :]
            if step != 0:
                extent = width + LANES
                g = pltpu.roll(jnp.concatenate([g, zeros(LANES)], axis=1), step % extent, 1)[:, :width]
            total = total + g
        held = total.astype(jnp.bfloat16).astype(jnp.float32)

    to_rows(flat, held)
    stage2[...] = flat[...].reshape(n, nt, LANES).astype(jnp.bfloat16)

    def result(p, send_at, recv_at, slot):
        return pltpu.make_async_remote_copy(
            src_ref=stage2.at[p],
            dst_ref=rbuf2.at[slot],
            send_sem=s_out.at[send_at],
            recv_sem=r_out.at[recv_at],
            device_id=(v, p),
            device_id_type=MESH,
        )

    def send_back(i, carry):
        p = lax.rem(me + i, n)
        result(p, i, me, me).start()
        return carry

    lax.fori_loop(1, n, send_back, 0)
    rbuf2[me] = stage2[me]

    def sent(i, carry):
        p = lax.rem(me + i, n)
        payload(p, i, p, p).wait_send()
        delay(v, p, 0, i, v, p).wait_send()
        delay(other, p, 1, i, v, p).wait_send()
        return carry

    delay(other, me, 1, 0, v, me).wait_send()
    lax.fori_loop(1, n, sent, 0)
    for it in range(ITERS):
        tail_copy(it).wait_send()

    def back(i, carry):
        p = lax.rem(me + i, n)
        result(p, i, p, p).wait_recv()
        result(p, i, p, p).wait_send()
        return carry

    lax.fori_loop(1, n, back, 0)
    flat[...] = rbuf2[...].astype(jnp.float32).reshape(n * nt, LANES)
    out_ref[0, 0] = from_rows(flat).astype(jnp.bfloat16)


def per_device(n, observed, estimate, delays, taps_time, taps_shot, thresh):
    receivers, width = observed.shape[1:]
    channels, taps = taps_time.shape
    assert observed.shape[0] == 1 and receivers == n and width % LANES == 0
    group = max(1, min(channels, 256 // n))
    chunks = channels // group
    rows = group * n
    depth = -(-taps * n // LANES) * LANES
    nt = width // LANES
    bf16, f32 = jnp.bfloat16, jnp.float32
    vmem = pl.BlockSpec(memory_space=pltpu.VMEM)
    dma = pltpu.SemaphoreType.DMA
    return pl.pallas_call(
        functools.partial(kernel, (n, width, channels, taps, chunks, rows, depth)),
        out_shape=jax.ShapeDtypeStruct(estimate.shape, bf16),
        in_specs=[vmem] * 6,
        out_specs=vmem,
        scratch_shapes=[
            pltpu.VMEM((n * nt, LANES), f32),
            pltpu.VMEM((n * nt, LANES), f32),
            pltpu.VMEM((n, 2, nt, LANES), bf16),
            pltpu.VMEM((n, 2, nt, LANES), bf16),
            pltpu.VMEM((1, LANES), jnp.int32),
            pltpu.VMEM((2, n, 1, LANES), jnp.int32),
            pltpu.VMEM((chunks, rows, depth), bf16),
            pltpu.VMEM((chunks, depth, rows), bf16),
            pltpu.VMEM((chunks, rows, 1), f32),
            pltpu.VMEM((depth, width), bf16),
            pltpu.VMEM((depth, width), f32),
            pltpu.VMEM((ITERS, n, MAXD), bf16),
            pltpu.VMEM((ITERS, n, MAXD), bf16),
            pltpu.VMEM((n, nt, LANES), bf16),
            pltpu.VMEM((n, nt, LANES), bf16),
            dma((n,)),
            dma((n,)),
            dma((2, n)),
            dma((2, n)),
            dma((ITERS,)),
            dma((ITERS,)),
            dma((n,)),
            dma((n,)),
        ],
        compiler_params=pltpu.CompilerParams(collective_id=0, has_side_effects=True),
    )(estimate, observed, delays, taps_time, taps_shot, thresh.reshape(1, channels))


def solution(mesh):
    return jax.shard_map(
        functools.partial(per_device, mesh.shape["gather"]),
        mesh=mesh,
        in_specs=(
            P("gather", None, None),
            P("vessel", "gather", None, None),
            P("vessel", "gather"),
            P(),
            P(),
            P(),
        ),
        out_specs=P("vessel", "gather", None, None),
        check_vma=False,
    )
```

```python
import functools

import jax
import jax.numpy as jnp
from jax import lax
from jax.experimental import pallas as pl
from jax.experimental.pallas import tpu as pltpu
from jax.sharding import PartitionSpec as P

TIME_SPACING = 4
SHOT_SPACING = 2
MAXD = 256
ITERS = 2
LANES = 128
REACH = 3

MESH = pl.DeviceIdType.MESH


def across(column, extent):
    return jnp.concatenate([column] * (extent // LANES), axis=1)


def shift_left(padded, amount, width, top):
    def bit_of(step, extent):
        bit = ((amount & step) != 0).astype(jnp.float32).astype(jnp.bfloat16)
        return across(bit, extent) > 0

    current = padded
    step = top
    keep = top
    while step >= LANES:
        bit = bit_of(step, width + keep)
        current = jnp.where(bit, current[:, step : step + width + keep], current[:, : width + keep])
        step //= 2
        keep = step
    extent = width + LANES
    current = current[:, :extent]
    while step >= 1:
        bit = bit_of(step, extent)
        current = jnp.where(bit, pltpu.roll(current, extent - step, 1), current)
        step //= 2
    return current[:, :width]


def kernel(
    dims,
    x_hbm,
    obs_hbm,
    d_hbm,
    tt_hbm,
    ts_hbm,
    th_hbm,
    out_ref,
    x_ref,
    obs_ref,
    d_ref,
    tt_ref,
    ts_ref,
    th_ref,
    s_in,
    flat,
    flat2,
    stage,
    rbuf,
    dsend,
    drecv,
    m_s,
    mt_s,
    th_s,
    pst,
    g_s,
    tail_s,
    tail_r,
    stage2,
    rbuf2,
    s_pay,
    r_pay,
    s_del,
    r_del,
    s_tail,
    r_tail,
    s_out,
    r_out,
):
    n, width, channels, taps, chunks, rows, depth = dims
    v = lax.axis_index("vessel")
    me = lax.axis_index("gather")
    other = 1 - v
    nt = width // LANES
    group = rows // n

    barrier = pltpu.get_barrier_semaphore()

    def greet(i, carry):
        p = lax.rem(me + i, n)
        pl.semaphore_signal(barrier, inc=1, device_id=(v, p), device_id_type=MESH)
        pl.semaphore_signal(barrier, inc=1, device_id=(other, p), device_id_type=MESH)
        return carry

    lax.fori_loop(1, n, greet, 0)
    pl.semaphore_signal(barrier, inc=1, device_id=(other, me), device_id_type=MESH)

    loads = [
        pltpu.make_async_copy(source, target, s_in.at[i])
        for i, (source, target) in enumerate(
            (
                (x_hbm, x_ref),
                (obs_hbm, obs_ref),
                (d_hbm, d_ref),
                (tt_hbm, tt_ref),
                (ts_hbm, ts_ref),
                (th_hbm, th_ref),
            )
        )
    ]
    for load in loads:
        load.start()
    for load in loads[:3]:
        load.wait()

    def to_rows(ref, value):
        for i in range(nt):
            ref[pl.ds(i, n, stride=nt), :] = value[:, i * LANES : (i + 1) * LANES]

    def from_rows(ref):
        return jnp.concatenate([ref[pl.ds(i, n, stride=nt), :] for i in range(nt)], axis=1)

    to_rows(flat, x_ref[0, 0].astype(jnp.float32))
    to_rows(flat2, obs_ref[0].astype(jnp.float32))
    stage[:, 0] = flat[...].reshape(n, nt, LANES).astype(jnp.bfloat16)
    stage[:, 1] = flat2[...].reshape(n, nt, LANES).astype(jnp.bfloat16)
    dsend[...] = jnp.broadcast_to(d_ref[...], (1, LANES))

    pl.semaphore_wait(barrier, 2 * n - 1)

    def payload(p, send_at, recv_at, slot):
        return pltpu.make_async_remote_copy(
            src_ref=stage.at[p],
            dst_ref=rbuf.at[slot],
            send_sem=s_pay.at[send_at],
            recv_sem=r_pay.at[recv_at],
            device_id=(v, p),
            device_id_type=MESH,
        )

    def delay(to_vessel, p, side, send_at, vessel_at, shot_at):
        return pltpu.make_async_remote_copy(
            src_ref=dsend,
            dst_ref=drecv.at[vessel_at, shot_at],
            send_sem=s_del.at[side, send_at],
            recv_sem=r_del.at[vessel_at, shot_at],
            device_id=(to_vessel, p),
            device_id_type=MESH,
        )

    delay(other, me, 1, 0, v, me).start()

    def send(i, carry):
        p = lax.rem(me + i, n)
        payload(p, i, me, me).start()
        delay(v, p, 0, i, v, me).start()
        delay(other, p, 1, i, v, me).start()
        return carry

    lax.fori_loop(1, n, send, 0)
    rbuf[me] = stage[me]
    drecv[v, me] = dsend[...]

    for load in loads[3:]:
        load.wait()

    def build(q, carry):
        row_ch = q * group + lax.broadcasted_iota(jnp.int32, (rows, channels), 0) // n
        pick = row_ch == lax.broadcasted_iota(jnp.int32, (rows, channels), 1)
        pick_f = pick.astype(jnp.float32)
        tt = lax.dot_general(pick_f, tt_ref[...], (((1,), (1,)), ((), ())), precision=lax.Precision.HIGHEST, preferred_element_type=jnp.float32)
        ts = lax.dot_general(pick_f, ts_ref[...], (((1,), (1,)), ((), ())), precision=lax.Precision.HIGHEST, preferred_element_type=jnp.float32)
        th_s[q] = jnp.broadcast_to(jnp.sum(jnp.where(pick, th_ref[...], 0.0), axis=1, keepdims=True), (rows, LANES))
        col = lax.broadcasted_iota(jnp.int32, (rows, depth), 1)
        row = lax.broadcasted_iota(jnp.int32, (rows, depth), 0)
        apart = lax.rem(col, n) - lax.rem(row, n)
        tap_of = col // n
        a = jnp.zeros((rows, depth), jnp.float32)
        b = jnp.zeros((rows, depth), jnp.float32)
        for k in range(taps):
            a = jnp.where(tap_of == k, tt[:, k : k + 1], a)
            b = jnp.where(apart == (k - REACH) * SHOT_SPACING, ts[:, k : k + 1], b)
        m = a * b
        m_s[q] = m.astype(jnp.bfloat16)
        mt_s[q] = m.T.astype(jnp.bfloat16)
        return carry

    if chunks == 1:
        build(0, 0)
    else:
        lax.fori_loop(0, chunks, build, 0)
    if depth > taps * n:
        pst[taps * n :, :] = jnp.zeros((depth - taps * n, width), jnp.bfloat16)

    def arrive(i, carry):
        p = lax.rem(me + i, n)
        payload(p, i, p, p).wait_recv()
        delay(v, p, 0, i, v, p).wait_recv()
        delay(v, p, 0, i, other, p).wait_recv()
        return carry

    delay(other, me, 1, 0, other, me).wait_recv()
    lax.fori_loop(1, n, arrive, 0)

    flat[...] = rbuf[:, 0].astype(jnp.float32).reshape(n * nt, LANES)
    flat2[...] = rbuf[:, 1].astype(jnp.float32).reshape(n * nt, LANES)
    held = from_rows(flat).astype(jnp.bfloat16)
    observed = from_rows(flat2).astype(jnp.bfloat16)
    d_mine = drecv[v].reshape(n, LANES)
    d_other = drecv[other].reshape(n, LANES)

    early_mark = width - 2 * MAXD
    block_width = 2048

    def filter_columns(start, stop):
        def one(q, first):
            for c0 in range(start, stop, block_width):
                c1 = min(c0 + block_width, stop)
                y = jnp.dot(m_s[q], pst[:, c0:c1], preferred_element_type=jnp.float32)
                th = across(th_s[q], c1 - c0)
                z = (y - jnp.minimum(jnp.maximum(y, -th), th)).astype(jnp.bfloat16)
                g = jnp.dot(mt_s[q], z, preferred_element_type=jnp.float32)
                if first:
                    g_s[:, c0:c1] = g
                else:
                    g_s[:, c0:c1] += g

        one(0, True)
        if chunks > 1:

            def more(q, carry):
                one(q, False)
                return carry

            lax.fori_loop(1, chunks, more, 0)

    def stack_taps(piece, lead, start, stop):
        extent = piece.shape[1]
        for k in range(taps):
            step = (k - REACH) * TIME_SPACING
            moved = piece if step == 0 else pltpu.roll(piece, (extent - step) % extent, 1)
            pst[k * n : (k + 1) * n, start:stop] = moved[:, lead : lead + stop - start]

    zeros = lambda w, t=jnp.bfloat16: jnp.zeros((n, w), t)

    def tail_copy(it):
        return pltpu.make_async_remote_copy(
            src_ref=tail_s.at[it],
            dst_ref=tail_r.at[it],
            send_sem=s_tail.at[it],
            recv_sem=r_tail.at[it],
            device_id=(other, me),
            device_id_type=MESH,
        )

    for it in range(ITERS):
        d_held, d_plane = (d_mine, d_other) if it % 2 == 0 else (d_other, d_mine)
        tail_s[it] = held[:, width - MAXD :]
        tail_copy(it).start()
        seen = shift_left(jnp.concatenate([observed, zeros(2 * MAXD)], axis=1), d_plane, width, MAXD)
        crossed = shift_left(
            jnp.concatenate([zeros(MAXD), held, zeros(3 * MAXD)], axis=1),
            d_plane - d_held + MAXD,
            width,
            2 * MAXD,
        )
        exact = seen.astype(jnp.float32) - crossed.astype(jnp.float32)
        plane = exact.astype(jnp.bfloat16)
        stack_taps(
            jnp.concatenate([plane[:, : early_mark + LANES], zeros(LANES)], axis=1), 0, 0, early_mark
        )
        filter_columns(0, early_mark)
        tail_copy(it).wait_recv()
        cut = width - MAXD
        time = cut + lax.broadcasted_iota(jnp.int32, (n, MAXD), 1)
        end = jnp.where(time + across(d_plane, MAXD) < width, exact[:, cut:], tail_r[it].astype(jnp.float32))
        end = end.astype(jnp.bfloat16)
        stack_taps(
            jnp.concatenate([plane[:, early_mark - LANES : cut], end, zeros(LANES)], axis=1),
            LANES,
            early_mark,
            width,
        )
        filter_columns(early_mark, width)
        total = zeros(width, jnp.float32)
        for k in range(taps):
            step = (k - REACH) * TIME_SPACING
            g = g_s[k * n : (k + 1) * n, :]
            if step != 0:
                extent = width + LANES
                g = pltpu.roll(jnp.concatenate([g, zeros(LANES, jnp.float32)], axis=1), step % extent, 1)[:, :width]
            total = total + g
        held = total.astype(jnp.bfloat16)

    to_rows(flat, held.astype(jnp.float32))
    stage2[...] = flat[...].reshape(n, nt, LANES).astype(jnp.bfloat16)

    def result(p, send_at, recv_at, slot):
        return pltpu.make_async_remote_copy(
            src_ref=stage2.at[p],
            dst_ref=rbuf2.at[slot],
            send_sem=s_out.at[send_at],
            recv_sem=r_out.at[recv_at],
            device_id=(v, p),
            device_id_type=MESH,
        )

    def send_back(i, carry):
        p = lax.rem(me + i, n)
        result(p, i, me, me).start()
        return carry

    lax.fori_loop(1, n, send_back, 0)
    rbuf2[me] = stage2[me]

    def sent(i, carry):
        p = lax.rem(me + i, n)
        payload(p, i, p, p).wait_send()
        delay(v, p, 0, i, v, p).wait_send()
        delay(other, p, 1, i, v, p).wait_send()
        return carry

    delay(other, me, 1, 0, v, me).wait_send()
    lax.fori_loop(1, n, sent, 0)
    for it in range(ITERS):
        tail_copy(it).wait_send()

    def back(i, carry):
        p = lax.rem(me + i, n)
        result(p, i, p, p).wait_recv()
        result(p, i, p, p).wait_send()
        return carry

    lax.fori_loop(1, n, back, 0)
    flat[...] = rbuf2[...].astype(jnp.float32).reshape(n * nt, LANES)
    out_ref[0, 0] = from_rows(flat).astype(jnp.bfloat16)


def per_device(n, observed, estimate, delays, taps_time, taps_shot, thresh):
    receivers, width = observed.shape[1:]
    channels, taps = taps_time.shape
    assert observed.shape[0] == 1 and receivers == n and width % LANES == 0
    group = max(1, min(channels, 256 // n))
    chunks = channels // group
    rows = group * n
    depth = -(-taps * n // LANES) * LANES
    nt = width // LANES
    bf16, f32 = jnp.bfloat16, jnp.float32
    vmem = pl.BlockSpec(memory_space=pltpu.VMEM)
    dma = pltpu.SemaphoreType.DMA
    return pl.pallas_call(
        functools.partial(kernel, (n, width, channels, taps, chunks, rows, depth)),
        out_shape=jax.ShapeDtypeStruct(estimate.shape, bf16),
        in_specs=[pl.BlockSpec(memory_space=pl.ANY)] * 6,
        out_specs=vmem,
        scratch_shapes=[
            pltpu.VMEM((1, 1, n, width), bf16),
            pltpu.VMEM((1, n, width), bf16),
            pltpu.VMEM((1, 1), jnp.int32),
            pltpu.VMEM((taps, channels), f32),
            pltpu.VMEM((taps, channels), f32),
            pltpu.VMEM((1, channels), f32),
            dma((6,)),
            pltpu.VMEM((n * nt, LANES), f32),
            pltpu.VMEM((n * nt, LANES), f32),
            pltpu.VMEM((n, 2, nt, LANES), bf16),
            pltpu.VMEM((n, 2, nt, LANES), bf16),
            pltpu.VMEM((1, LANES), jnp.int32),
            pltpu.VMEM((2, n, 1, LANES), jnp.int32),
            pltpu.VMEM((chunks, rows, depth), bf16),
            pltpu.VMEM((chunks, depth, rows), bf16),
            pltpu.VMEM((chunks, rows, LANES), f32),
            pltpu.VMEM((depth, width), bf16),
            pltpu.VMEM((depth, width), f32),
            pltpu.VMEM((ITERS, n, MAXD), bf16),
            pltpu.VMEM((ITERS, n, MAXD), bf16),
            pltpu.VMEM((n, nt, LANES), bf16),
            pltpu.VMEM((n, nt, LANES), bf16),
            dma((n,)),
            dma((n,)),
            dma((2, n)),
            dma((2, n)),
            dma((ITERS,)),
            dma((ITERS,)),
            dma((n,)),
            dma((n,)),
        ],
        compiler_params=pltpu.CompilerParams(collective_id=0, has_side_effects=True),
    )(estimate, observed, delays, taps_time.T, taps_shot.T, thresh.reshape(1, channels))


def solution(mesh):
    return jax.shard_map(
        functools.partial(per_device, mesh.shape["gather"]),
        mesh=mesh,
        in_specs=(
            P("gather", None, None),
            P("vessel", "gather", None, None),
            P("vessel", "gather"),
            P(),
            P(),
            P(),
        ),
        out_specs=P("vessel", "gather", None, None),
        check_vma=False,
    )
```

```python
import functools

import jax
import jax.numpy as jnp
from jax import lax
from jax.experimental import pallas as pl
from jax.experimental.pallas import tpu as pltpu
from jax.sharding import PartitionSpec as P

TIME_SPACING = 4
SHOT_SPACING = 2
MAXD = 256
ITERS = 2
LANES = 128
REACH = 3

MESH = pl.DeviceIdType.MESH


def partner_of(me, i, n):
    return me ^ (n - i) if n & (n - 1) == 0 else lax.rem(me + i, n)


def across(column, extent):
    return jnp.concatenate([column] * (extent // LANES), axis=1)


def shift_left(padded, amount, width, top):
    def choose(step, moved, kept):
        bit = ((amount & step) != 0).astype(jnp.float32)
        extent = moved.shape[1]
        taken = across(bit.astype(jnp.bfloat16), extent)
        left = across((1.0 - bit).astype(jnp.bfloat16), extent)
        return moved * taken + kept * left

    current = padded
    step = top
    keep = top
    while step >= LANES:
        current = choose(step, current[:, step : step + width + keep], current[:, : width + keep])
        step //= 2
        keep = step
    extent = width + LANES
    current = current[:, :extent]
    while step >= 1:
        current = choose(step, pltpu.roll(current, extent - step, 1), current)
        step //= 2
    return current[:, :width]


def kernel(
    dims,
    x_hbm,
    obs_hbm,
    d_hbm,
    tt_hbm,
    ts_hbm,
    th_hbm,
    out_ref,
    x_ref,
    obs_ref,
    d_ref,
    tt_ref,
    ts_ref,
    th_ref,
    s_in,
    flat,
    flat2,
    stage,
    rbuf,
    dsend,
    drecv,
    m_s,
    mt_s,
    th_s,
    pst,
    g_s,
    tail_s,
    tail_r,
    stage2,
    rbuf2,
    s_pay,
    r_pay,
    s_del,
    r_del,
    s_tail,
    r_tail,
    s_out,
    r_out,
):
    n, width, channels, taps, chunks, rows, depth = dims
    v = lax.axis_index("vessel")
    me = lax.axis_index("gather")
    other = 1 - v
    nt = width // LANES
    group = rows // n

    barrier = pltpu.get_barrier_semaphore()

    def greet(i, carry):
        p = lax.rem(me + i, n)
        pl.semaphore_signal(barrier, inc=1, device_id=(v, p), device_id_type=MESH)
        pl.semaphore_signal(barrier, inc=1, device_id=(other, p), device_id_type=MESH)
        return carry

    lax.fori_loop(1, n, greet, 0)
    pl.semaphore_signal(barrier, inc=1, device_id=(other, me), device_id_type=MESH)

    loads = [
        pltpu.make_async_copy(source, target, s_in.at[i])
        for i, (source, target) in enumerate(
            (
                (x_hbm, x_ref),
                (obs_hbm, obs_ref),
                (d_hbm, d_ref),
                (tt_hbm, tt_ref),
                (ts_hbm, ts_ref),
                (th_hbm, th_ref),
            )
        )
    ]
    for load in loads:
        load.start()
    for load in loads[:3]:
        load.wait()

    def to_rows(ref, value):
        for i in range(nt):
            ref[pl.ds(i, n, stride=nt), :] = value[:, i * LANES : (i + 1) * LANES]

    def from_rows(ref):
        return jnp.concatenate([ref[pl.ds(i, n, stride=nt), :] for i in range(nt)], axis=1)

    to_rows(flat, x_ref[0, 0].astype(jnp.float32))
    to_rows(flat2, obs_ref[0].astype(jnp.float32))
    stage[:, 0] = flat[...].reshape(n, nt, LANES).astype(jnp.bfloat16)
    stage[:, 1] = flat2[...].reshape(n, nt, LANES).astype(jnp.bfloat16)
    dsend[...] = jnp.broadcast_to(d_ref[...], (1, LANES))

    pl.semaphore_wait(barrier, 2 * n - 1)

    def payload(p, send_at, recv_at, slot):
        return pltpu.make_async_remote_copy(
            src_ref=stage.at[p],
            dst_ref=rbuf.at[slot],
            send_sem=s_pay.at[send_at],
            recv_sem=r_pay.at[recv_at],
            device_id=(v, p),
            device_id_type=MESH,
        )

    def delay(to_vessel, p, side, send_at, vessel_at, shot_at):
        return pltpu.make_async_remote_copy(
            src_ref=dsend,
            dst_ref=drecv.at[vessel_at, shot_at],
            send_sem=s_del.at[side, send_at],
            recv_sem=r_del.at[vessel_at, shot_at],
            device_id=(to_vessel, p),
            device_id_type=MESH,
        )

    def send(i, carry):
        p = partner_of(me, i, n)
        payload(p, i, me, me).start()
        return carry

    def send_delay(i, carry):
        p = partner_of(me, i, n)
        delay(v, p, 0, i, v, me).start()
        delay(other, p, 1, i, v, me).start()
        return carry

    lax.fori_loop(1, n, send, 0)
    lax.fori_loop(1, n, send_delay, 0)
    delay(other, me, 1, 0, v, me).start()
    rbuf[me] = stage[me]
    drecv[v, me] = dsend[...]

    for load in loads[3:]:
        load.wait()

    def build(q, carry):
        row_ch = q * group + lax.broadcasted_iota(jnp.int32, (rows, channels), 0) // n
        pick = row_ch == lax.broadcasted_iota(jnp.int32, (rows, channels), 1)
        pick_f = pick.astype(jnp.float32)
        tt = lax.dot_general(pick_f, tt_ref[...], (((1,), (1,)), ((), ())), precision=lax.Precision.HIGHEST, preferred_element_type=jnp.float32)
        ts = lax.dot_general(pick_f, ts_ref[...], (((1,), (1,)), ((), ())), precision=lax.Precision.HIGHEST, preferred_element_type=jnp.float32)
        th_s[q] = jnp.broadcast_to(jnp.sum(jnp.where(pick, th_ref[...], 0.0), axis=1, keepdims=True), (rows, LANES))
        col = lax.broadcasted_iota(jnp.int32, (rows, depth), 1)
        row = lax.broadcasted_iota(jnp.int32, (rows, depth), 0)
        apart = lax.rem(col, n) - lax.rem(row, n)
        tap_of = col // n
        a = jnp.zeros((rows, depth), jnp.float32)
        b = jnp.zeros((rows, depth), jnp.float32)
        for k in range(taps):
            a = jnp.where(tap_of == k, tt[:, k : k + 1], a)
            b = jnp.where(apart == (k - REACH) * SHOT_SPACING, ts[:, k : k + 1], b)
        m = a * b
        m_s[q] = m.astype(jnp.bfloat16)
        mt_s[q] = m.T.astype(jnp.bfloat16)
        return carry

    if chunks == 1:
        build(0, 0)
    else:
        lax.fori_loop(0, chunks, build, 0)
    if depth > taps * n:
        pst[taps * n :, :] = jnp.zeros((depth - taps * n, width), jnp.bfloat16)

    def arrive(i, carry):
        p = partner_of(me, i, n)
        payload(p, i, p, p).wait_recv()
        delay(v, p, 0, i, v, p).wait_recv()
        delay(v, p, 0, i, other, p).wait_recv()
        return carry

    delay(other, me, 1, 0, other, me).wait_recv()
    lax.fori_loop(1, n, arrive, 0)

    flat[...] = rbuf[:, 0].astype(jnp.float32).reshape(n * nt, LANES)
    flat2[...] = rbuf[:, 1].astype(jnp.float32).reshape(n * nt, LANES)
    held = from_rows(flat).astype(jnp.bfloat16)
    observed = from_rows(flat2).astype(jnp.bfloat16)
    d_mine = drecv[v].reshape(n, LANES)
    d_other = drecv[other].reshape(n, LANES)

    early_mark = width - 2 * MAXD
    block_width = 2048

    def filter_columns(start, stop):
        def one(q, first):
            for c0 in range(start, stop, block_width):
                c1 = min(c0 + block_width, stop)
                y = jnp.dot(m_s[q], pst[:, c0:c1], preferred_element_type=jnp.float32)
                th = across(th_s[q], c1 - c0)
                z = (y - jnp.minimum(jnp.maximum(y, -th), th)).astype(jnp.bfloat16)
                g = jnp.dot(mt_s[q], z, preferred_element_type=jnp.float32)
                if first:
                    g_s[:, c0:c1] = g
                else:
                    g_s[:, c0:c1] += g

        one(0, True)
        if chunks > 1:

            def more(q, carry):
                one(q, False)
                return carry

            lax.fori_loop(1, chunks, more, 0)

    def stack_taps(piece, lead, start, stop):
        extent = piece.shape[1]
        for k in range(taps):
            step = (k - REACH) * TIME_SPACING
            moved = piece if step == 0 else pltpu.roll(piece, (extent - step) % extent, 1)
            pst[k * n : (k + 1) * n, start:stop] = moved[:, lead : lead + stop - start]

    zeros = lambda w, t=jnp.bfloat16: jnp.zeros((n, w), t)

    def tail_copy(it):
        return pltpu.make_async_remote_copy(
            src_ref=tail_s.at[it],
            dst_ref=tail_r.at[it],
            send_sem=s_tail.at[it],
            recv_sem=r_tail.at[it],
            device_id=(other, me),
            device_id_type=MESH,
        )

    for it in range(ITERS):
        d_held, d_plane = (d_mine, d_other) if it % 2 == 0 else (d_other, d_mine)
        tail_s[it] = held[:, width - MAXD :]
        tail_copy(it).start()
        seen = shift_left(jnp.concatenate([observed, zeros(2 * MAXD)], axis=1), d_plane, width, MAXD)
        crossed = shift_left(
            jnp.concatenate([zeros(MAXD), held, zeros(3 * MAXD)], axis=1),
            d_plane - d_held + MAXD,
            width,
            2 * MAXD,
        )
        exact = seen.astype(jnp.float32) - crossed.astype(jnp.float32)
        plane = exact.astype(jnp.bfloat16)
        stack_taps(
            jnp.concatenate([plane[:, : early_mark + LANES], zeros(LANES)], axis=1), 0, 0, early_mark
        )
        filter_columns(0, early_mark)
        tail_copy(it).wait_recv()
        cut = width - MAXD
        time = cut + lax.broadcasted_iota(jnp.int32, (n, MAXD), 1)
        end = jnp.where(time + across(d_plane, MAXD) < width, exact[:, cut:], tail_r[it].astype(jnp.float32))
        end = end.astype(jnp.bfloat16)
        stack_taps(
            jnp.concatenate([plane[:, early_mark - LANES : cut], end, zeros(LANES)], axis=1),
            LANES,
            early_mark,
            width,
        )
        filter_columns(early_mark, width)
        total = zeros(width, jnp.float32)
        for k in range(taps):
            step = (k - REACH) * TIME_SPACING
            g = g_s[k * n : (k + 1) * n, :]
            if step != 0:
                extent = width + LANES
                g = pltpu.roll(jnp.concatenate([g, zeros(LANES, jnp.float32)], axis=1), step % extent, 1)[:, :width]
            total = total + g
        held = total.astype(jnp.bfloat16)

    to_rows(flat, held.astype(jnp.float32))
    stage2[...] = flat[...].reshape(n, nt, LANES).astype(jnp.bfloat16)

    def result(p, send_at, recv_at, slot):
        return pltpu.make_async_remote_copy(
            src_ref=stage2.at[p],
            dst_ref=rbuf2.at[slot],
            send_sem=s_out.at[send_at],
            recv_sem=r_out.at[recv_at],
            device_id=(v, p),
            device_id_type=MESH,
        )

    def send_back(i, carry):
        p = partner_of(me, i, n)
        result(p, i, me, me).start()
        return carry

    lax.fori_loop(1, n, send_back, 0)
    rbuf2[me] = stage2[me]

    def sent(i, carry):
        p = partner_of(me, i, n)
        payload(p, i, p, p).wait_send()
        delay(v, p, 0, i, v, p).wait_send()
        delay(other, p, 1, i, v, p).wait_send()
        return carry

    delay(other, me, 1, 0, v, me).wait_send()
    lax.fori_loop(1, n, sent, 0)
    for it in range(ITERS):
        tail_copy(it).wait_send()

    def back(i, carry):
        p = partner_of(me, i, n)
        result(p, i, p, p).wait_recv()
        result(p, i, p, p).wait_send()
        return carry

    lax.fori_loop(1, n, back, 0)
    flat[...] = rbuf2[...].astype(jnp.float32).reshape(n * nt, LANES)
    out_ref[0, 0] = from_rows(flat).astype(jnp.bfloat16)


def per_device(n, observed, estimate, delays, taps_time, taps_shot, thresh):
    receivers, width = observed.shape[1:]
    channels, taps = taps_time.shape
    assert observed.shape[0] == 1 and receivers == n and width % LANES == 0
    group = max(1, min(channels, 256 // n))
    chunks = channels // group
    rows = group * n
    depth = -(-taps * n // LANES) * LANES
    nt = width // LANES
    bf16, f32 = jnp.bfloat16, jnp.float32
    vmem = pl.BlockSpec(memory_space=pltpu.VMEM)
    dma = pltpu.SemaphoreType.DMA
    operands = (estimate, observed, delays, taps_time.T, taps_shot.T, thresh.reshape(1, channels))
    operands = [
        operand if operand is delays else pltpu.with_memory_space_constraint(operand, pltpu.HBM)
        for operand in operands
    ]
    return pl.pallas_call(
        functools.partial(kernel, (n, width, channels, taps, chunks, rows, depth)),
        out_shape=pltpu.VMEM(estimate.shape, bf16),
        in_specs=[pl.BlockSpec(memory_space=pl.ANY)] * 6,
        out_specs=vmem,
        scratch_shapes=[
            pltpu.VMEM((1, 1, n, width), bf16),
            pltpu.VMEM((1, n, width), bf16),
            pltpu.VMEM((1, 1), jnp.int32),
            pltpu.VMEM((taps, channels), f32),
            pltpu.VMEM((taps, channels), f32),
            pltpu.VMEM((1, channels), f32),
            dma((6,)),
            pltpu.VMEM((n * nt, LANES), f32),
            pltpu.VMEM((n * nt, LANES), f32),
            pltpu.VMEM((n, 2, nt, LANES), bf16),
            pltpu.VMEM((n, 2, nt, LANES), bf16),
            pltpu.VMEM((1, LANES), jnp.int32),
            pltpu.VMEM((2, n, 1, LANES), jnp.int32),
            pltpu.VMEM((chunks, rows, depth), bf16),
            pltpu.VMEM((chunks, depth, rows), bf16),
            pltpu.VMEM((chunks, rows, LANES), f32),
            pltpu.VMEM((depth, width), bf16),
            pltpu.VMEM((depth, width), f32),
            pltpu.VMEM((ITERS, n, MAXD), bf16),
            pltpu.VMEM((ITERS, n, MAXD), bf16),
            pltpu.VMEM((n, nt, LANES), bf16),
            pltpu.VMEM((n, nt, LANES), bf16),
            dma((n,)),
            dma((n,)),
            dma((2, n)),
            dma((2, n)),
            dma((ITERS,)),
            dma((ITERS,)),
            dma((n,)),
            dma((n,)),
        ],
        compiler_params=pltpu.CompilerParams(collective_id=0, has_side_effects=True, vmem_limit_bytes=48 << 20),
        )(*operands)


def solution(mesh):
    return jax.shard_map(
        functools.partial(per_device, mesh.shape["gather"]),
        mesh=mesh,
        in_specs=(
            P("gather", None, None),
            P("vessel", "gather", None, None),
            P("vessel", "gather"),
            P(),
            P(),
            P(),
        ),
        out_specs=P("vessel", "gather", None, None),
        check_vma=False,
    )
```
